32 devices in a mesh: grid: 8 (over z, x), chan: 4 (over y, core).
Axes of the slice: x: 2, y: 2, z: 4, core: 2. Of those that a mesh axis runs over, the one named last changes fastest.
Arguments:
- volt: float32 [2, 128, 4096, 512], P(None, None, 'grid', 'chan'), may hold values from -13 to 13
- placement: int32 [4096], P('grid'), may hold values from 0 to 63, as said below
- flags: int32 [4096], P('grid'), may hold values 0 or 1
Outputs:
- sky_image: float32 [64, 64], P('chan', 'grid')
The draws below stay inside these ranges and needn't reach their ends.
Inputs may be any that keep to these rules, and one draw needn't show every extreme that they name: `placement`: within every grid row r, antennas r * 64 to (r + 1) * 64 - 1 take each column 0 to 63 exactly once.
All inputs are finite; a program needn't handle non-finite values. No bound on the sum of `flags` on one device may be relied on, other than what follows from the above.
Results may differ from the reference program's by a relative error of at most 0.0001.
Values sent between devices are 32-bit elements; how exact they have to be, the bound alone decides.
No kernel may reach another device: no remote copies, remote signals or barrier semaphores. Data moves between devices by JAX's collectives and lax.ppermute only.
A program may use at most 320 MiB of HBM per device.

```python
import math
import jax
import jax.numpy as jnp
from jax import lax

NROW = 64
GRID_COLUMNS = 64
CHANNELS = 512
TIMES = 128
ANTENNAS = 4096


source_count = 16


def place_map(key):
    row_keys = jax.random.split(jax.random.fold_in(key, 7), NROW)
    row_perm = jax.vmap(lambda row_key: jax.random.permutation(row_key, GRID_COLUMNS))(row_keys)
    return row_perm.astype(jnp.int32).reshape(ANTENNAS)


def draw_placement(key, part):
    return place_map(key)


def draw_volt(key, part):
    place_col = place_map(key)
    grid_row = jnp.arange(ANTENNAS, dtype=jnp.int32) // GRID_COLUMNS
    base = jax.random.fold_in(key, 9)
    key_row, key_col, key_amp, key_sig, key_noise = jax.random.split(base, 5)
    src_row = jax.random.randint(key_row, (source_count,), 0, NROW)
    src_col = jax.random.randint(key_col, (source_count,), 0, GRID_COLUMNS)
    src_amp = jnp.exp(jax.random.uniform(key_amp, (source_count,), jnp.float32, math.log(0.03), math.log(0.1)))
    src_signal = jnp.clip(jax.random.normal(key_sig, (2, TIMES, CHANNELS, source_count), jnp.float32), -4.0, 4.0)
    src_signal = src_signal * (src_amp / math.sqrt(2.0))
    row_part = (grid_row[:, None] * src_row[None, :] % NROW).astype(jnp.float32) / NROW
    col_part = (place_col[:, None] * src_col[None, :] % GRID_COLUMNS).astype(jnp.float32) / GRID_COLUMNS
    src_phase = 2.0 * math.pi * (row_part + col_part)
    phase_cosine = jnp.cos(src_phase)
    phase_sine = jnp.sin(src_phase)
    signal_real = src_signal[0]
    signal_imaginary = src_signal[1]
    real_component = jnp.einsum('ybd,zd->yzb', signal_real, phase_cosine) - jnp.einsum('ybd,zd->yzb', signal_imaginary, phase_sine)
    imaginary_component = jnp.einsum('ybd,zd->yzb', signal_real, phase_sine) + jnp.einsum('ybd,zd->yzb', signal_imaginary, phase_cosine)
    noise_part = jnp.clip(jax.random.normal(key_noise, (2, TIMES, ANTENNAS, CHANNELS), jnp.float32), -6.0, 6.0)
    return (jnp.stack([real_component, imaginary_component]) + noise_part).astype(jnp.float32)


def place_ends(values, rng, least, largest):
    spot = [jax.random.randint(jax.random.fold_in(rng, axis), (), 0, length) for axis, length in enumerate(values.shape)]
    longest = values.shape.index(max(values.shape))
    next_to = spot[:longest] + [(spot[longest] + 1) % values.shape[longest]] + spot[longest + 1:]
    return values.at[tuple(spot)].set(least).at[tuple(next_to)].set(largest)


def setup_inputs(seed: int = 0) -> dict:
    key_of = jax.random.split(jax.random.key(seed), 4)
    volt = draw_volt(jax.random.fold_in(key_of[3], 71), 0)
    placement = draw_placement(jax.random.fold_in(key_of[3], 71), 0)
    flags = place_ends((jax.random.randint(key_of[2], (ANTENNAS,), 0, 4) < 3).astype(jnp.int32), jax.random.fold_in(key_of[2], 1), 0, 1)
    return dict(volt=volt, placement=placement, flags=flags)


def reference(volt, placement, flags):
    columns = jnp.arange(GRID_COLUMNS, dtype=jnp.int32)
    onehot = (placement[:, None] == columns[None, :]).astype(jnp.float32) * flags[:, None].astype(jnp.float32)
    onehot = onehot.reshape(NROW, GRID_COLUMNS, GRID_COLUMNS)

    def one_sample(step, running):
        sample = lax.dynamic_index_in_dim(volt, step, 1, keepdims=False)
        gridded = sample.reshape(2, NROW, GRID_COLUMNS, CHANNELS)
        sky_cells = jnp.einsum("sxac,xay->sxyc", gridded, onehot, precision=lax.Precision.HIGHEST)
        spectrum = jnp.fft.fft2(sky_cells[0] + 1j * sky_cells[1], axes=(0, 1))
        return running + jnp.sum(jnp.real(spectrum) ** 2 + jnp.imag(spectrum) ** 2, axis=2)

    running = lax.fori_loop(0, TIMES, one_sample, jnp.zeros((NROW, GRID_COLUMNS), jnp.float32))
    return running * (1.0 / (TIMES * CHANNELS * NROW * GRID_COLUMNS))
```

```python
import functools
import math

import jax
import jax.numpy as jnp
from jax import lax
from jax.experimental import pallas as pl
from jax.experimental.pallas import tpu as pltpu
from jax.sharding import PartitionSpec as P

NROW = 64
GRID_COLUMNS = 64
CHANNELS = 512
TIMES = 128
SUB = 8
QUANTUM = 32


def cosine(phase, length):
    turned = (phase % length).astype(jnp.float32) * (2.0 * math.pi / length)
    return jnp.cos(turned)


def halves(value):
    high = value.astype(jnp.bfloat16)
    low = (value - high.astype(jnp.float32)).astype(jnp.bfloat16)
    return high, low


def constant_halves(value):
    high = lax.reduce_precision(value, exponent_bits=8, mantissa_bits=7)
    return high.astype(jnp.bfloat16), (value - high).astype(jnp.bfloat16)


def mm(left, right):
    return jnp.dot(left, right, preferred_element_type=jnp.float32)


def pack_kernel(slots, first_ref, where_ref, volt_ref, out_ref):
    del first_ref
    ants = where_ref.shape[1]
    chans = volt_ref.shape[3]
    slot_ids = lax.broadcasted_iota(jnp.int32, (slots, ants), 0)
    pick = (slot_ids == where_ref[...]).astype(jnp.float32).astype(jnp.bfloat16)
    both = jnp.concatenate([volt_ref[0, 0], volt_ref[1, 0]], axis=1)
    high, low = halves(both)
    kept = mm(pick, high) + mm(pick, low)
    out_ref[0, 0, 0] = kept[:, :chans]
    out_ref[0, 0, 1] = kept[:, chans:]


def pack(volt, where, slots, group, first, count):
    _, samples, ants, chans = volt.shape
    per_dest = samples // group
    return pl.pallas_call(
        functools.partial(pack_kernel, slots),
        grid_spec=pltpu.PrefetchScalarGridSpec(
            num_scalar_prefetch=1,
            grid=(group, count),
            in_specs=[
                pl.BlockSpec((1, ants), lambda g, j, first: (0, 0)),
                pl.BlockSpec((2, 1, ants, chans), lambda g, j, first: (0, g * per_dest + first[0] + j, 0, 0)),
            ],
            out_specs=pl.BlockSpec((1, 1, 2, slots, chans), lambda g, j, first: (g, j, 0, 0, 0)),
        ),
        out_shape=jax.ShapeDtypeStruct((group, count, 2, slots, chans), jnp.float32),
        cost_estimate=pl.CostEstimate(
            flops=group * count * slots * ants * chans * 8,
            bytes_accessed=group * count * 8 * chans * (ants + slots),
            transcendentals=0,
        ),
        name="pack",
    )(jnp.full((1,), first, jnp.int32), where, volt)


def table_kernel(wave_high_ref, wave_low_ref, row_ref, term_ref, high_ref, low_ref):
    lines, terms = wave_high_ref.shape
    depth = row_ref.shape[2]
    rows = high_ref.shape[1] // lines
    hit = term_ref[0] == lax.broadcasted_iota(jnp.int32, (terms, depth), 0)
    hit = hit.astype(jnp.float32).astype(jnp.bfloat16)
    mine = row_ref[0] == lax.broadcasted_iota(jnp.int32, (rows, depth), 0)
    for wave_ref, out_ref in ((wave_high_ref, high_ref), (wave_low_ref, low_ref)):
        wave = mm(wave_ref[...], hit)
        spread = jnp.where(mine[None], wave[:, None, :], 0.0)
        out_ref[0] = spread.reshape(lines * rows, depth).astype(jnp.bfloat16)


def tables(wave_high, wave_low, row, term, rows):
    lines = wave_high.shape[0]
    groups, _, depth = row.shape
    out = jax.ShapeDtypeStruct((groups, lines * rows, depth), jnp.bfloat16)
    spec = pl.BlockSpec((1, lines * rows, depth), lambda d: (d, 0, 0))
    slot_spec = pl.BlockSpec((1, 1, depth), lambda d: (d, 0, 0))
    wave_spec = pl.BlockSpec(wave_high.shape, lambda d: (0, 0))
    return pl.pallas_call(
        table_kernel,
        grid=(groups,),
        in_specs=[wave_spec, wave_spec, slot_spec, slot_spec],
        out_specs=(spec, spec),
        out_shape=(out, out),
        cost_estimate=pl.CostEstimate(
            flops=groups * lines * rows * depth * 4,
            bytes_accessed=groups * lines * rows * depth * 4,
            transcendentals=0,
        ),
        name="tables",
    )(wave_high, wave_low, row, term)


def image_kernel(rows, got_ref, high_ref, low_ref, col_ref, acc_in_ref, acc_ref, mid_ref):
    step = pl.program_id(1)
    count = got_ref.shape[1]
    chans = got_ref.shape[4]
    depth = high_ref.shape[2]
    lines = high_ref.shape[1] // rows
    sides = [got_ref[:, j].reshape(depth, chans) for j in range(count)]
    data = jnp.concatenate(sides, axis=1) if count > 1 else sides[0]
    high, low = halves(data)
    some = 32

    def part(i, carry):
        span = pl.ds(pl.multiple_of(i * some * rows, some * rows), some * rows)
        coarse = high_ref[0, span, :]
        fine = low_ref[0, span, :]
        found = mm(coarse, high) + mm(coarse, low) + mm(fine, high)
        mid_ref[pl.ds(i * some, some), pl.ds(pl.multiple_of(step * rows, rows), rows), :] = found.reshape(
            some, rows, count * chans
        )
        return carry

    lax.fori_loop(0, lines // some, part, 0)

    @pl.when((step == 0) & (pl.program_id(0) == 0))
    def _():
        acc_ref[...] = acc_in_ref[...]

    @pl.when(step == pl.num_programs(1) - 1)
    def _():
        half = col_ref.shape[0] // 2

        def column(v, carry):
            line = mid_ref[pl.ds(2 * v, 2)].reshape(2 * mid_ref.shape[1], count * chans)
            line_high, line_low = halves(line)
            seen = mm(col_ref[...], jnp.concatenate([line_high, line_low, line_high], axis=0))
            seen = seen * seen
            power = seen[:half] + seen[half:]
            total = power[:, :chans]
            for j in range(1, count):
                total = total + power[:, j * chans : (j + 1) * chans]
            acc_ref[v] += total
            return carry

        lax.fori_loop(0, lines // 2, column, 0, unroll=4)


def image(got, high, low, col, acc, rows):
    sources, count, _, slots, chans = got.shape
    groups, tall, depth = high.shape
    each = sources // groups
    lines = tall // rows
    block = 2 if count % 2 == 0 else 1
    whole_acc = pl.BlockSpec(acc.shape, lambda p, d: (0, 0, 0))
    table_spec = pl.BlockSpec((1, tall, depth), lambda p, d: (d, 0, 0))
    return pl.pallas_call(
        functools.partial(image_kernel, rows),
        grid=(count // block, groups),
        in_specs=[
            pl.BlockSpec((each, block, 2, slots, chans), lambda p, d: (d, p, 0, 0, 0)),
            table_spec,
            table_spec,
            pl.BlockSpec(col.shape, lambda p, d: (0, 0)),
            whole_acc,
        ],
        out_specs=whole_acc,
        out_shape=jax.ShapeDtypeStruct(acc.shape, jnp.float32),
        scratch_shapes=[pltpu.VMEM((lines, groups * rows, block * chans), jnp.float32)],
        cost_estimate=pl.CostEstimate(
            flops=6 * groups * tall * depth * count * chans,
            bytes_accessed=4 * got.size + 4 * high.size + 8 * acc.size,
            transcendentals=0,
        ),
        name="image",
    )(got, high, low, col, acc)


def chunk_sizes(samples):
    if samples < 8 or samples % 8:
        return [samples]
    piece = samples // 8
    return [piece, 3 * piece, 3 * piece, piece]


def share(value, axes, size):
    return lax.all_to_all(jnp.broadcast_to(value[None], (size,) + value.shape), axes, 0, 0, tiled=True)


def on_device(group, others, volt, placement, flags):
    _, samples, ants, chans = volt.shape
    local_rows = ants // GRID_COLUMNS
    per_dest = samples // group
    each = max(1, SUB // local_rows)
    groups = group // each
    rows = local_rows * each

    codes = share(placement * 2 + flags, "grid", group)
    used = codes % 2
    upto = lax.broadcasted_iota(jnp.int32, (ants, ants), 0) <= lax.broadcasted_iota(jnp.int32, (ants, ants), 1)
    place = jnp.dot(
        used.astype(jnp.bfloat16), upto.astype(jnp.bfloat16), preferred_element_type=jnp.float32
    ).astype(jnp.int32)
    most = jnp.max(place[:, -1])
    where = jnp.where(used == 1, place - 1, -1)
    mine = lax.dynamic_slice_in_dim(where, lax.axis_index("grid"), 1, axis=0)
    cell = codes // 2 + lax.broadcasted_iota(jnp.int32, (group, ants), 1) // GRID_COLUMNS * GRID_COLUMNS + 1

    quarter = NROW // 4
    shape = (2 * NROW, 2 * NROW)
    line_ids = lax.broadcasted_iota(jnp.int32, shape, 0)
    term_ids = lax.broadcasted_iota(jnp.int32, shape, 1)
    turn = quarter * (term_ids // NROW)
    col_high, col_low = constant_halves(
        cosine((line_ids % NROW) * (term_ids % NROW) + quarter * (line_ids // NROW) - turn, NROW)
    )
    col = jnp.concatenate([col_high, col_high, col_low], axis=1)
    wave_high, wave_low = constant_halves(
        cosine((line_ids // 2) * (term_ids % NROW) + quarter * (line_ids % 2) - turn, NROW)
    )

    def with_slots(slots):
        def run(volt, where, mine, cell, col, wave_high, wave_low):
            hit = where[:, None, :] == lax.broadcasted_iota(jnp.int32, (1, slots, 1), 1)
            tag = jnp.sum(jnp.where(hit, cell[:, None, :], 0), axis=2) - 1
            slot_row = jnp.where(tag >= 0, tag // GRID_COLUMNS, -rows)
            slot_row = slot_row + lax.broadcasted_iota(jnp.int32, (group, slots), 0) % each * local_rows
            slot_col = tag % GRID_COLUMNS
            depth = each * 2 * slots
            twice = lambda a, b: jnp.stack([a, b], axis=1).reshape(groups, 1, depth)
            high, low = tables(
                wave_high,
                wave_low,
                twice(slot_row, slot_row),
                twice(slot_col, slot_col + GRID_COLUMNS),
                rows,
            )
            chunks = chunk_sizes(per_dest)
            acc = jnp.zeros((GRID_COLUMNS, NROW, chans), jnp.float32)
            packed = pack(volt, mine, slots, group, 0, chunks[0])
            first = chunks[0]
            behind = None
            for i in range(len(chunks)):
                got = lax.all_to_all(packed, "grid", split_axis=0, concat_axis=0, tiled=True)
                if behind is not None:
                    acc = image(behind, high, low, col, acc, rows)
                if i + 1 < len(chunks):
                    mine, acc = lax.optimization_barrier((mine, acc))
                    packed = pack(volt, mine, slots, group, first, chunks[i + 1])
                    first += chunks[i + 1]
                behind = got
            acc = image(behind, high, low, col, acc, rows)
            return jnp.sum(acc, axis=2)

        return run

    quantum = min(QUANTUM, ants)
    sizes = BUCKETS if BUCKETS else list(range(quantum, ants + 1, quantum))
    which = jnp.clip((most + quantum - 1) // quantum - 1, 0, len(sizes) - 1)
    power = lax.switch(
        which, [with_slots(s) for s in sizes], volt, where, mine, cell, col, wave_high, wave_low
    )
    blocks = power.T.reshape(others, NROW // others, group, GRID_COLUMNS // group)
    blocks = blocks.transpose(2, 0, 1, 3).reshape(group * others, -1)
    parts = lax.all_to_all(blocks, ("grid", "chan"), split_axis=0, concat_axis=0, tiled=True)
    summed = jnp.sum(parts, axis=0).reshape(NROW // others, GRID_COLUMNS // group)
    return summed * (1.0 / (TIMES * CHANNELS * NROW * GRID_COLUMNS))


BUCKETS = None


def solution(mesh):
    return jax.shard_map(
        functools.partial(on_device, mesh.shape["grid"], mesh.shape["chan"]),
        mesh=mesh,
        in_specs=(P(None, None, "grid", "chan"), P("grid"), P("grid")),
        out_specs=P("chan", "grid"),
        check_vma=False,
    )
```

```python
import functools
import math

import jax
import jax.numpy as jnp
from jax import lax
from jax.experimental import pallas as pl
from jax.experimental.pallas import tpu as pltpu
from jax.sharding import PartitionSpec as P

NROW = 64
GRID_COLUMNS = 64
CHANNELS = 512
TIMES = 128
SUB = 8
QUANTUM = 16


def cosine(phase, length):
    turned = (phase % length).astype(jnp.float32) * (2.0 * math.pi / length)
    return jnp.cos(turned)


def halves(value):
    high = value.astype(jnp.bfloat16)
    low = (value - high.astype(jnp.float32)).astype(jnp.bfloat16)
    return high, low


def constant_halves(value):
    high = lax.reduce_precision(value, exponent_bits=8, mantissa_bits=7)
    return high.astype(jnp.bfloat16), (value - high).astype(jnp.bfloat16)


def mm(left, right):
    return jnp.dot(left, right, preferred_element_type=jnp.float32)


def pack_kernel(slots, first_ref, where_ref, volt_ref, out_ref):
    del first_ref
    ants = where_ref.shape[1]
    chans = volt_ref.shape[3]
    slot_ids = lax.broadcasted_iota(jnp.int32, (slots, ants), 0)
    pick = (slot_ids == where_ref[...]).astype(jnp.float32).astype(jnp.bfloat16)
    both = jnp.concatenate([volt_ref[0, 0], volt_ref[1, 0]], axis=1)
    high, low = halves(both)
    kept = mm(pick, high) + mm(pick, low)
    out_ref[0, 0, 0] = kept[:, :chans]
    out_ref[0, 0, 1] = kept[:, chans:]


def pack(volt, where, slots, group, first, count):
    _, samples, ants, chans = volt.shape
    per_dest = samples // group
    return pl.pallas_call(
        functools.partial(pack_kernel, slots),
        grid_spec=pltpu.PrefetchScalarGridSpec(
            num_scalar_prefetch=1,
            grid=(group, count),
            in_specs=[
                pl.BlockSpec((1, ants), lambda g, j, first: (0, 0)),
                pl.BlockSpec((2, 1, ants, chans), lambda g, j, first: (0, g * per_dest + first[0] + j, 0, 0)),
            ],
            out_specs=pl.BlockSpec((1, 1, 2, slots, chans), lambda g, j, first: (g, j, 0, 0, 0)),
        ),
        out_shape=jax.ShapeDtypeStruct((group, count, 2, slots, chans), jnp.float32),
        cost_estimate=pl.CostEstimate(
            flops=group * count * slots * ants * chans * 8,
            bytes_accessed=group * count * 8 * chans * (ants + slots),
            transcendentals=0,
        ),
        name="pack",
    )(jnp.full((1,), first, jnp.int32), where, volt)


def table_kernel(wave_high_ref, wave_low_ref, row_ref, term_ref, high_ref, low_ref):
    lines, terms = wave_high_ref.shape
    depth = row_ref.shape[2]
    rows = high_ref.shape[1] // lines
    hit = term_ref[0] == lax.broadcasted_iota(jnp.int32, (terms, depth), 0)
    hit = hit.astype(jnp.float32).astype(jnp.bfloat16)
    mine = row_ref[0] == lax.broadcasted_iota(jnp.int32, (rows, depth), 0)
    for wave_ref, out_ref in ((wave_high_ref, high_ref), (wave_low_ref, low_ref)):
        wave = mm(wave_ref[...], hit)
        spread = jnp.where(mine[None], wave[:, None, :], 0.0)
        out_ref[0] = spread.reshape(lines * rows, depth).astype(jnp.bfloat16)


def tables(wave_high, wave_low, row, term, rows):
    lines = wave_high.shape[0]
    groups, _, depth = row.shape
    out = jax.ShapeDtypeStruct((groups, lines * rows, depth), jnp.bfloat16)
    spec = pl.BlockSpec((1, lines * rows, depth), lambda d: (d, 0, 0))
    slot_spec = pl.BlockSpec((1, 1, depth), lambda d: (d, 0, 0))
    wave_spec = pl.BlockSpec(wave_high.shape, lambda d: (0, 0))
    return pl.pallas_call(
        table_kernel,
        grid=(groups,),
        in_specs=[wave_spec, wave_spec, slot_spec, slot_spec],
        out_specs=(spec, spec),
        out_shape=(out, out),
        cost_estimate=pl.CostEstimate(
            flops=groups * lines * rows * depth * 4,
            bytes_accessed=groups * lines * rows * depth * 4,
            transcendentals=0,
        ),
        name="tables",
    )(wave_high, wave_low, row, term)


def image_kernel(rows, got_ref, high_ref, low_ref, col_ref, acc_in_ref, acc_ref, mid_ref):
    step = pl.program_id(1)
    count = got_ref.shape[1]
    chans = got_ref.shape[4]
    depth = high_ref.shape[2]
    lines = high_ref.shape[1] // rows
    sides = [got_ref[:, j].reshape(depth, chans) for j in range(count)]
    data = jnp.concatenate(sides, axis=1) if count > 1 else sides[0]
    high, low = halves(data)
    some = 32

    def part(i, carry):
        span = pl.ds(pl.multiple_of(i * some * rows, some * rows), some * rows)
        coarse = high_ref[0, span, :]
        fine = low_ref[0, span, :]
        found = mm(coarse, high) + mm(coarse, low) + mm(fine, high)
        mid_ref[pl.ds(i * some, some), pl.ds(pl.multiple_of(step * rows, rows), rows), :] = found.reshape(
            some, rows, count * chans
        )
        return carry

    lax.fori_loop(0, lines // some, part, 0)

    @pl.when((step == 0) & (pl.program_id(0) == 0))
    def _():
        acc_ref[...] = acc_in_ref[...]

    @pl.when(step == pl.num_programs(1) - 1)
    def _():
        half = col_ref.shape[0] // 2

        def column(v, carry):
            line = mid_ref[pl.ds(2 * v, 2)].reshape(2 * mid_ref.shape[1], count * chans)
            line_high, line_low = halves(line)
            seen = mm(col_ref[...], jnp.concatenate([line_high, line_low, line_high], axis=0))
            seen = seen * seen
            power = seen[:half] + seen[half:]
            total = power[:, :chans]
            for j in range(1, count):
                total = total + power[:, j * chans : (j + 1) * chans]
            acc_ref[v] += total
            return carry

        lax.fori_loop(0, lines // 2, column, 0, unroll=4)


def image(got, high, low, col, acc, rows):
    sources, count, _, slots, chans = got.shape
    groups, tall, depth = high.shape
    each = sources // groups
    lines = tall // rows
    block = 2 if count % 2 == 0 else 1
    whole_acc = pl.BlockSpec(acc.shape, lambda p, d: (0, 0, 0))
    table_spec = pl.BlockSpec((1, tall, depth), lambda p, d: (d, 0, 0))
    return pl.pallas_call(
        functools.partial(image_kernel, rows),
        grid=(count // block, groups),
        in_specs=[
            pl.BlockSpec((each, block, 2, slots, chans), lambda p, d: (d, p, 0, 0, 0)),
            table_spec,
            table_spec,
            pl.BlockSpec(col.shape, lambda p, d: (0, 0)),
            whole_acc,
        ],
        out_specs=whole_acc,
        out_shape=jax.ShapeDtypeStruct(acc.shape, jnp.float32),
        scratch_shapes=[pltpu.VMEM((lines, groups * rows, block * chans), jnp.float32)],
        cost_estimate=pl.CostEstimate(
            flops=6 * groups * tall * depth * count * chans,
            bytes_accessed=4 * got.size + 4 * high.size + 8 * acc.size,
            transcendentals=0,
        ),
        name="image",
    )(got, high, low, col, acc)


def chunk_sizes(samples):
    if samples < 8 or samples % 8:
        return [samples]
    piece = samples // 8
    return [piece, 3 * piece, 3 * piece, piece]


def capacities(ants):
    sizes, size = [ants], ants
    while True:
        step = max(QUANTUM, size // 32 // QUANTUM * QUANTUM)
        step = step if size > ants // 2 else 2 * step
        if size - step < QUANTUM or size - step < ants // 16:
            return sizes[::-1]
        size -= step
        sizes.append(size)


def share(value, axes, size):
    return lax.all_to_all(jnp.broadcast_to(value[None], (size,) + value.shape), axes, 0, 0, tiled=True)


def on_device(group, others, volt, placement, flags):
    _, samples, ants, chans = volt.shape
    local_rows = ants // GRID_COLUMNS
    per_dest = samples // group
    each = max(1, SUB // local_rows)
    groups = group // each
    rows = local_rows * each

    upto = lax.broadcasted_iota(jnp.int32, (ants, ants), 0) <= lax.broadcasted_iota(jnp.int32, (ants, ants), 1)

    def slot_of(used):
        place = jnp.dot(
            used.astype(jnp.bfloat16), upto.astype(jnp.bfloat16), preferred_element_type=jnp.float32
        ).astype(jnp.int32)
        return place, jnp.where(used == 1, place - 1, -1)

    codes = share(placement * 2 + flags, "grid", group)
    _, mine = slot_of(flags[None])
    chunks = chunk_sizes(per_dest)
    packed_wide = pack(volt, mine, ants, group, 0, chunks[0])
    place, where = slot_of(codes % 2)
    most = jnp.max(place[:, -1])
    cell = codes // 2 + lax.broadcasted_iota(jnp.int32, (group, ants), 1) // GRID_COLUMNS * GRID_COLUMNS + 1

    quarter = NROW // 4
    shape = (2 * NROW, 2 * NROW)
    line_ids = lax.broadcasted_iota(jnp.int32, shape, 0)
    term_ids = lax.broadcasted_iota(jnp.int32, shape, 1)
    turn = quarter * (term_ids // NROW)
    col_high, col_low = constant_halves(
        cosine((line_ids % NROW) * (term_ids % NROW) + quarter * (line_ids // NROW) - turn, NROW)
    )
    col = jnp.concatenate([col_high, col_high, col_low], axis=1)
    wave_high, wave_low = constant_halves(
        cosine((line_ids // 2) * (term_ids % NROW) + quarter * (line_ids % 2) - turn, NROW)
    )

    def with_slots(slots):
        def run(volt, packed_wide, where, mine, cell, col, wave_high, wave_low):
            hit = where[:, None, :] == lax.broadcasted_iota(jnp.int32, (1, slots, 1), 1)
            tag = jnp.sum(jnp.where(hit, cell[:, None, :], 0), axis=2) - 1
            slot_row = jnp.where(tag >= 0, tag // GRID_COLUMNS, -rows)
            slot_row = slot_row + lax.broadcasted_iota(jnp.int32, (group, slots), 0) % each * local_rows
            slot_col = tag % GRID_COLUMNS
            depth = each * 2 * slots
            twice = lambda a, b: jnp.stack([a, b], axis=1).reshape(groups, 1, depth)
            high, low = tables(
                wave_high,
                wave_low,
                twice(slot_row, slot_row),
                twice(slot_col, slot_col + GRID_COLUMNS),
                rows,
            )
            acc = jnp.zeros((GRID_COLUMNS, NROW, chans), jnp.float32)
            packed = packed_wide[:, :, :, :slots]
            first = chunks[0]
            behind = None
            for i in range(len(chunks)):
                got = lax.all_to_all(packed, "grid", split_axis=0, concat_axis=0, tiled=True)
                if behind is not None:
                    acc = image(behind, high, low, col, acc, rows)
                if i + 1 < len(chunks):
                    mine, acc = lax.optimization_barrier((mine, acc))
                    packed = pack(volt, mine, slots, group, first, chunks[i + 1])
                    first += chunks[i + 1]
                behind = got
            acc = image(behind, high, low, col, acc, rows)
            return jnp.sum(acc, axis=2)

        return run

    sizes = BUCKETS if BUCKETS else capacities(ants)
    which = jnp.sum(jnp.array(sizes[:-1], jnp.int32) < most) if len(sizes) > 1 else 0
    power = lax.switch(
        which, [with_slots(s) for s in sizes], volt, packed_wide, where, mine, cell, col, wave_high, wave_low
    )
    blocks = power.T.reshape(others, NROW // others, group, GRID_COLUMNS // group)
    blocks = blocks.transpose(2, 0, 1, 3).reshape(group * others, -1)
    parts = lax.all_to_all(blocks, ("grid", "chan"), split_axis=0, concat_axis=0, tiled=True)
    summed = jnp.sum(parts, axis=0).reshape(NROW // others, GRID_COLUMNS // group)
    return summed * (1.0 / (TIMES * CHANNELS * NROW * GRID_COLUMNS))


BUCKETS = None


def solution(mesh):
    return jax.shard_map(
        functools.partial(on_device, mesh.shape["grid"], mesh.shape["chan"]),
        mesh=mesh,
        in_specs=(P(None, None, "grid", "chan"), P("grid"), P("grid")),
        out_specs=P("chan", "grid"),
        check_vma=False,
    )
```
